256 devices in a mesh: samples: 64 (over z, y, x_lo), vblocks: 4 (over x_hi, core).
Axes of the slice: x: 4 (x_hi: 2, x_lo: 2; x = x_hi * 2 + x_lo), y: 4, z: 8, core: 2. Of those that a mesh axis runs over, the one named last changes fastest.
Arguments:
- genotypes: int32 [65536, 4096], P('samples', 'vblocks'), may hold values from 0 to 2
- typed_mask: int32 [4096], P('vblocks'), may hold values 0 or 1
- z_scores: float32 [1024, 4096], P('samples', 'vblocks'), may hold values from -60 to 60
Outputs:
- solution: float32 [1024, 4096], P('samples', 'vblocks')
- imputed: float32 [1024, 4096], P('samples', 'vblocks')
The draws below stay inside these ranges and needn't reach their ends.
All inputs are finite; a program needn't handle non-finite values. No bound on the sum of `typed_mask` on one device may be relied on, other than what follows from the above.
Results may differ from the reference program's by a relative error of at most 0.0068.
Values may be sent and summed in bfloat16 or wider, within the bound.
No kernel may reach another device: no remote copies, remote signals or barrier semaphores. Data moves between devices by JAX's collectives and lax.ppermute only.
A program may use at most 64 MiB of HBM per device.

```python
import math
import jax
import jax.numpy as jnp
from jax import lax

BAND = 1024
ITERS = 3
S = 65536
V = 4096
K = 1024
N_VBLOCKS = 4


def haplotype(key_hap, thresholds):
    key_draw, key_copy = jax.random.split(key_hap)
    uniform_draw = jax.random.randint(key_draw, (S, V), 0, 100)
    copied = jax.random.randint(key_copy, (S, V), 0, 10) < 9
    position = lax.broadcasted_iota(jnp.int32, (S, V), 1)
    fresh_start = jnp.logical_or(jnp.logical_not(copied), position == 0)
    source = lax.cummax(jnp.where(fresh_start, position, 0), axis=1)
    carried = jnp.take_along_axis(uniform_draw, source, axis=1)
    return (carried < thresholds).astype(jnp.int32)


def draw_genotypes(key, part):
    key_freq, key_first, key_second = jax.random.split(key, 3)
    percent = jax.random.randint(key_freq, (V,), 1, 34)
    sample_index = lax.broadcasted_iota(jnp.int32, (S, V), 0)
    thresholds = percent[None, :] * (S + 2 * sample_index) // S
    return haplotype(key_first, thresholds) + haplotype(key_second, thresholds)


def draw_z_scores(key, part):
    key_base, key_rows, key_cols = jax.random.split(key, 3)
    spread = math.log(10.0) / 2.0
    row_scale = jnp.exp(jax.random.uniform(key_rows, (1, V), jnp.float32, -spread, spread))
    col_scale = jnp.exp(jax.random.uniform(key_cols, (K, 1), jnp.float32, -spread, spread))
    base_draw = jax.random.truncated_normal(key_base, -6.0, 6.0, (K, V), jnp.float32)
    return (base_draw * row_scale * col_scale).astype(jnp.float32)


def touch_ends(array, rng, smallest, largest):
    index_at = [jax.random.randint(jax.random.fold_in(rng, axis), (), 0, length) for axis, length in enumerate(array.shape)]
    main_axis = array.shape.index(max(array.shape))
    neighbour = index_at[:main_axis] + [(index_at[main_axis] + 1) % array.shape[main_axis]] + index_at[main_axis + 1:]
    return array.at[tuple(index_at)].set(smallest).at[tuple(neighbour)].set(largest)


def setup_inputs(seed: int = 0) -> dict:
    keys = jax.random.split(jax.random.key(seed), 4)
    genotypes = draw_genotypes(jax.random.fold_in(keys[3], 71), 0)
    typed_mask = touch_ends((jax.random.randint(keys[1], (V,), 0, 4) < 3).astype(jnp.int32), jax.random.fold_in(keys[1], 1), 0, 1)
    z_scores = draw_z_scores(jax.random.fold_in(keys[3], 71), 0)
    return dict(genotypes=genotypes, typed_mask=typed_mask, z_scores=z_scores)


RIDGE = 0.1
EPSILON = 1e-05
HIGHEST = lax.Precision.HIGHEST

def contract_rows(first_mat, second_mat):
    return lax.dot_general(first_mat, second_mat, (((0,), (0,)), ((), ())), preferred_element_type=jnp.float32)

def times_transpose(vector, matrix):
    return lax.dot_general(vector, matrix, (((1,), (1,)), ((), ())), precision=HIGHEST, preferred_element_type=jnp.float32)

def apply_link(vector, own_blocks, edge_blocks):
    pieces = [vector[:, block_index * BAND:(block_index + 1) * BAND] for block_index in range(N_VBLOCKS)]
    outputs = []
    for block_index in range(N_VBLOCKS):
        result = times_transpose(pieces[block_index], own_blocks[block_index])
        if block_index + 1 < N_VBLOCKS:
            result = result + 0.5 * times_transpose(pieces[block_index + 1], edge_blocks[block_index])
        if block_index > 0:
            result = result + 0.5 * jnp.dot(pieces[block_index - 1], edge_blocks[block_index - 1], precision=HIGHEST, preferred_element_type=jnp.float32)
        outputs.append(result)
    return jnp.concatenate(outputs, axis=1)

def rounded_link(first_mat, second_mat, samples):
    summed = (contract_rows(first_mat, second_mat) / samples).astype(jnp.bfloat16)
    return lax.optimization_barrier(summed).astype(jnp.float32)

def reference(genotypes, typed_mask, z_scores):
    samples = genotypes.shape[0]
    standard_blocks = []
    for block_index in range(N_VBLOCKS):
        dosage = genotypes[:, block_index * BAND:(block_index + 1) * BAND].astype(jnp.float32)
        totals = lax.optimization_barrier(jnp.sum(dosage, axis=0))
        squares = lax.optimization_barrier(jnp.sum(dosage * dosage, axis=0))
        mean_dosage = totals / samples
        variance = squares / samples - mean_dosage * mean_dosage
        standard_blocks.append(((dosage - mean_dosage) * lax.rsqrt(variance + EPSILON)).astype(jnp.bfloat16))
    own_blocks = []
    edge_blocks = []
    for block_index in range(N_VBLOCKS):
        own_blocks.append(rounded_link(standard_blocks[block_index], standard_blocks[block_index], samples))
        if block_index + 1 < N_VBLOCKS:
            edge_blocks.append(rounded_link(standard_blocks[block_index], standard_blocks[block_index + 1], samples))
        else:
            edge_blocks.append(jnp.zeros((BAND, BAND), jnp.float32))
    mask_row = typed_mask.astype(jnp.float32)[None, :]

    def operator(vector):
        return mask_row * apply_link(mask_row * vector, own_blocks, edge_blocks) + RIDGE * vector
    right_side = mask_row * z_scores
    solution = jnp.zeros_like(right_side)
    residual = right_side
    direction = right_side
    norm_now = lax.optimization_barrier(jnp.sum(residual * residual, axis=1))
    for iteration in range(ITERS):
        image = operator(direction)
        step_size = norm_now / lax.optimization_barrier(jnp.sum(direction * image, axis=1))
        solution = solution + step_size[:, None] * direction
        residual = residual - step_size[:, None] * image
        if iteration + 1 < ITERS:
            norm_next = lax.optimization_barrier(jnp.sum(residual * residual, axis=1))
            direction = residual + (norm_next / norm_now)[:, None] * direction
            norm_now = norm_next
    projected = apply_link(mask_row * solution, own_blocks, edge_blocks)
    imputed = jnp.where(typed_mask[None, :] == 1, z_scores, projected)
    return (solution, imputed)
```

```python
import jax
import jax.numpy as jnp
from jax import lax
from jax.sharding import Mesh, PartitionSpec as P

ITERS = 3
RIDGE = 0.1
EPSILON = 1e-05
HIGHEST = lax.Precision.HIGHEST
BF16 = jnp.bfloat16
F32 = jnp.float32

SAMPLE_AXES = ("z", "y", "xl")
BLOCK_AXES = ("xh", "core")
N_BLOCKS = 4


def from_next(block):
    return lax.ppermute(block, BLOCK_AXES, [(i + 1, i) for i in range(N_BLOCKS - 1)])


def from_previous(block):
    return lax.ppermute(block, BLOCK_AXES, [(i, i + 1) for i in range(N_BLOCKS - 1)])


def contract_rows(first_mat, second_mat):
    return lax.dot_general(
        first_mat, second_mat, (((0,), (0,)), ((), ())), preferred_element_type=F32
    )


def rounded(values):
    return lax.reduce_precision(values, exponent_bits=8, mantissa_bits=7)


def split3(vector):
    high = rounded(vector)
    rest = vector - high
    mid = rounded(rest)
    return jnp.concatenate([high, mid, rest - mid], axis=0).astype(BF16)


def join3(stacked):
    rows = stacked.shape[0] // 3
    return stacked[2 * rows :] + stacked[rows : 2 * rows] + stacked[:rows]


def times(vector, matrix, side):
    out = lax.dot_general(
        split3(vector), matrix, (((1,), (side,)), ((), ())), preferred_element_type=F32
    )
    return join3(out)


def gather_stats(local_sums, local_squares):
    sums, squares = local_sums, local_squares
    for axis in ("z", "y", "xl"):
        packed = jnp.concatenate([sums, squares], axis=0)[None]
        packed = lax.all_gather(packed, axis, axis=0, tiled=True)
        sums = packed[:, :-1].reshape(-1, packed.shape[-1])
        squares = jnp.sum(packed[:, -1], axis=0, keepdims=True)
    return sums, squares


def line_of(all_sums, all_squares, total_samples):
    coded_sum = jnp.sum(all_sums, axis=0, keepdims=True)
    mean_dosage = (coded_sum + total_samples) / total_samples
    squares = all_squares + 2.0 * coded_sum + total_samples
    variance = squares / total_samples - mean_dosage * mean_dosage
    scale = lax.rsqrt(variance + EPSILON)
    twos = 0.5 * (all_squares + coded_sum)
    zeros = 0.5 * (all_squares - coded_sum)
    ones = total_samples - all_squares
    level = rise = spread = 0.0
    for dosage, count in ((0.0, zeros), (1.0, ones), (2.0, twos)):
        away = dosage - mean_dosage
        value = rounded(away * scale)
        level = level + count * value
        rise = rise + count * value * away
        spread = spread + count * away * away
    slope = jnp.where(spread > 0.0, rise / jnp.where(spread > 0.0, spread, 1.0), scale)
    return level / total_samples, slope


def on_device(genotypes, typed_mask, z_scores):
    samples_dev, width = genotypes.shape
    n_dev = lax.axis_size(SAMPLE_AXES)
    total_samples = samples_dev * n_dev
    coded = (genotypes - 1).astype(BF16)
    following = from_next(coded)
    joined = jnp.concatenate([coded, following], axis=1)
    joined_f = joined.astype(F32)
    sums = jnp.sum(joined_f, axis=0, keepdims=True)
    squares = jnp.sum(joined_f * joined_f, axis=0, keepdims=True)
    counts = contract_rows(coded, joined)
    centred = (counts - sums[0, :width, None] * (sums / samples_dev)).astype(BF16)

    within = lax.psum_scatter(centred, "z", scatter_dimension=0, tiled=True)
    within = lax.psum_scatter(within.astype(F32), "y", scatter_dimension=0, tiled=True)
    within = lax.psum_scatter(within, "xl", scatter_dimension=0, tiled=True)

    all_sums, all_squares = gather_stats(sums, squares)
    level, slope = line_of(all_sums, all_squares, total_samples)
    off = (all_sums - jnp.mean(all_sums, axis=0, keepdims=True)) * slope
    rows = within.shape[0]
    start = lax.axis_index(SAMPLE_AXES) * rows
    off_rows = lax.dynamic_slice_in_dim(off, start, rows, axis=1)
    slope_rows = lax.dynamic_slice_in_dim(slope, start, rows, axis=1)
    level_rows = lax.dynamic_slice_in_dim(level, start, rows, axis=1)
    between = lax.dot_general(
        off_rows, off, (((0,), (0,)), ((), ())), precision=HIGHEST, preferred_element_type=F32
    )
    link = (within * slope * slope_rows[0][:, None] + between / samples_dev) / total_samples
    link = link + level_rows[0][:, None] * level
    link_rows = link.astype(BF16)

    gathered = lax.all_gather(link_rows, "xl", axis=0, tiled=True)
    gathered = lax.all_gather(gathered, "y", axis=0, tiled=True)
    gathered = lax.all_gather(gathered, "z", axis=0, tiled=True)
    own_block = gathered[:, :width]
    edge_block = gathered[:, width:]

    def apply_link(vector):
        ahead_part = from_next(vector)
        outgoing = times(vector, edge_block, 0)
        lower_part = from_previous(outgoing)
        result = times(vector, own_block, 1)
        result = result + 0.5 * times(ahead_part, edge_block, 1)
        return result + 0.5 * lower_part

    def dots(*pairs):
        local = jnp.stack([jnp.sum(a * b, axis=1) for a, b in pairs])
        return lax.psum(local, BLOCK_AXES)

    mask_row = typed_mask.astype(F32)[None, :]
    right_side = mask_row * z_scores

    residual = right_side
    linked = apply_link(mask_row * residual)
    image = mask_row * linked + RIDGE * residual
    norm_now, curvature = dots((residual, residual), (residual, image))
    direction = residual
    step_size = (norm_now / curvature)[:, None]
    solution = step_size * direction
    projected = step_size * linked
    for iteration in range(1, ITERS):
        residual = residual - step_size * image
        fresh_link = apply_link(mask_row * residual)
        fresh_image = mask_row * fresh_link + RIDGE * residual
        norm_next, fresh_curve, cross_a, cross_b, old_curve = dots(
            (residual, residual),
            (residual, fresh_image),
            (residual, image),
            (direction, fresh_image),
            (direction, image),
        )
        ratio = norm_next / norm_now
        curvature = fresh_curve + ratio * (cross_a + cross_b) + ratio * ratio * old_curve
        step_size = (norm_next / curvature)[:, None]
        direction = residual + ratio[:, None] * direction
        image = fresh_image + ratio[:, None] * image
        linked = fresh_link + ratio[:, None] * linked
        solution = solution + step_size * direction
        projected = projected + step_size * linked
        norm_now = norm_next
    imputed = jnp.where(typed_mask[None, :] == 1, z_scores, projected)
    return (solution, imputed)


def solution(mesh):
    fine = Mesh(mesh.devices.reshape(8, 4, 2, 2, 2), SAMPLE_AXES + BLOCK_AXES)
    placed = (P(SAMPLE_AXES, BLOCK_AXES), P(BLOCK_AXES), P(SAMPLE_AXES, BLOCK_AXES))
    return jax.shard_map(
        on_device,
        mesh=fine,
        in_specs=placed,
        out_specs=(P(SAMPLE_AXES, BLOCK_AXES), P(SAMPLE_AXES, BLOCK_AXES)),
        check_vma=False,
    )
```

```python
import jax
import jax.numpy as jnp
from jax import lax
from jax.sharding import Mesh, PartitionSpec as P

ITERS = 3
RIDGE = 0.1
EPSILON = 1e-05
BF16 = jnp.bfloat16
F32 = jnp.float32

SAMPLE_AXES = ("z", "y", "xl")
BLOCK_AXES = ("xh", "core")
SOLVE_AXES = ("xl",) + BLOCK_AXES
SIZES = (8, 4, 2, 2, 2)
N_BLOCKS = 4


def shift(block, axis, distance):
    size = lax.axis_size(axis)
    return lax.ppermute(block, axis, [(i, (i + distance) % size) for i in range(size)])


def between_blocks(block, distance, cross):
    route = []
    for half in range(2):
        for i in range(N_BLOCKS):
            if 0 <= i + distance < N_BLOCKS:
                there = 1 - half if cross else half
                route.append((half * N_BLOCKS + i, there * N_BLOCKS + i + distance))
    return lax.ppermute(block, SOLVE_AXES, route)


def from_next(block):
    return between_blocks(block, -1, False)


def contract_rows(first_mat, second_mat):
    return lax.dot_general(
        first_mat, second_mat, (((0,), (0,)), ((), ())), preferred_element_type=F32
    )


def rounded(values):
    return lax.reduce_precision(values, exponent_bits=8, mantissa_bits=7)


def split3(vector):
    high = rounded(vector)
    rest = vector - high
    mid = rounded(rest)
    return jnp.concatenate([high, mid, rest - mid], axis=0).astype(BF16)


def times(stacked, matrix, side):
    out = lax.dot_general(
        stacked, matrix, (((1,), (side,)), ((), ())), preferred_element_type=F32
    )
    rows = stacked.shape[0] // 3
    return out[2 * rows :] + out[rows : 2 * rows] + out[:rows]


def add(first, second):
    return (first.astype(F32) + second.astype(F32)).astype(BF16)


def ring_reduce(parts, axis):
    size = lax.axis_size(axis)
    half = size // 2
    here = lax.axis_index(axis).astype(jnp.uint32)

    def part(offset):
        return lax.dynamic_index_in_dim(parts, (here + (offset + size)) & (size - 1), 1, keepdims=False)

    far = part(half)
    right, left = shift(far[:1], axis, 1), shift(far[1:], axis, -1)
    for offset in range(half - 1, 0, -1):
        ahead, behind = part(offset), part(-offset)
        if offset == half - 1:
            ahead = jnp.concatenate([add(ahead[:1], right), ahead[1:]], axis=0)
            behind = jnp.concatenate([behind[:1], add(behind[1:], left)], axis=0)
        else:
            ahead, behind = add(ahead, right), add(behind, left)
        right, left = shift(ahead, axis, 1), shift(behind, axis, -1)
    mine = part(0).astype(F32)
    if half == 1:
        return mine + jnp.concatenate([right, left], axis=0).astype(F32)
    return mine + right.astype(F32) + left.astype(F32)


def ring_gather(rows, axis):
    size = lax.axis_size(axis)
    half = size // 2
    here = lax.axis_index(axis).astype(jnp.uint32)
    out = jnp.zeros((size,) + rows.shape, rows.dtype)

    def place(whole, piece, offset):
        return lax.dynamic_update_index_in_dim(whole, piece, (here + (offset + size)) & (size - 1), 0)

    out = place(out, rows, 0)
    right = left = rows
    for offset in range(1, half):
        right, left = shift(right, axis, 1), shift(left, axis, -1)
        out = place(place(out, right, -offset), left, offset)
    cut = rows.shape[0] // 2
    far = jnp.concatenate([shift(right[:cut], axis, 1), shift(left[cut:], axis, -1)], axis=0)
    out = place(out, far, half)
    return out.reshape((size * rows.shape[0],) + rows.shape[1:])


def swap_halves(values, half):
    cut = values.shape[-1] // 2
    swapped = jnp.concatenate([values[..., cut:], values[..., :cut]], axis=-1)
    return jnp.where(half == 0, values, swapped)


def reduce_link(product, order, total_samples, half):
    width = product.shape[0]
    rows = product.astype(BF16)
    for axis in order:
        size = lax.axis_size(axis)
        rows = ring_reduce(rows.reshape(2, size, -1, width), axis).astype(BF16)
    mine = lax.dynamic_index_in_dim(rows, half, 0, keepdims=False)
    other = lax.dynamic_index_in_dim(rows, 1 - half, 0, keepdims=False)
    summed = mine.astype(F32) + shift(other, "xl", 1).astype(F32)
    return swap_halves((summed / total_samples).astype(BF16), half)


def sum_over(values, axes):
    for axis in axes:
        size = lax.axis_size(axis)
        if size > 2:
            values = values + shift(values, axis, size // 2)
            if size > 4:
                values = values + shift(values, axis, size // 4)
            values = values + shift(values, axis, 1)
        else:
            values = values + shift(values, axis, 1)
    return values


def on_device(genotypes, typed_mask, z_scores):
    samples_dev, width = genotypes.shape
    total_samples = samples_dev * lax.axis_size(SAMPLE_AXES)
    cut = width // 2
    half = lax.axis_index("xl").astype(jnp.uint32)

    coded = lax.optimization_barrier(genotypes.astype(BF16))
    following = from_next(coded)
    dosage = coded.astype(F32)
    sums = jnp.stack([jnp.sum(dosage, axis=0), jnp.sum(dosage * dosage, axis=0)])
    sums = sum_over(sums, SAMPLE_AXES)
    following_sums = from_next(sums)

    def standardize(values, both_sums):
        mean_dosage = both_sums[0] / total_samples
        variance = both_sums[1] / total_samples - mean_dosage * mean_dosage
        return ((values - mean_dosage) * lax.rsqrt(variance + EPSILON)).astype(BF16)

    standard = standardize(dosage, sums)
    own_rows = reduce_link(contract_rows(standard, standard), ("z", "y"), total_samples, half)
    next_standard = standardize(following.astype(F32), following_sums)
    edge_rows = reduce_link(
        contract_rows(standard, next_standard), ("y", "z"), total_samples, half
    )
    own = ring_gather(ring_gather(own_rows, "y"), "z")
    edge = ring_gather(ring_gather(edge_rows, "z"), "y")

    def apply_link(vector):
        partner = shift(vector, "xl", 1)
        ahead = jnp.concatenate(
            [between_blocks(vector, -1, False), between_blocks(vector, -1, True)], axis=1
        )
        mine = split3(vector)
        outgoing = times(mine, edge, 0)
        lower = between_blocks(outgoing[:, :cut], 1, False)
        lower = lower + between_blocks(outgoing[:, cut:], 1, True)
        both = jnp.concatenate([mine, split3(partner)], axis=1)
        result = times(both, own, 1) + 0.5 * times(split3(ahead), edge, 1)
        return result + 0.5 * lower

    def dots(*pairs):
        local = jnp.stack([jnp.sum(a * b, axis=1) for a, b in pairs])
        local = local + shift(local, "xl", 1)
        local = local + shift(local, "core", 1)
        return (local + shift(local, "xh", 1))[:, :, None]

    kept = lax.dynamic_slice_in_dim(z_scores, half * cut, cut, 1)
    sent = lax.dynamic_slice_in_dim(z_scores, (1 - half) * cut, cut, 1)
    taken = shift(sent, "xl", 1)
    scores = jnp.where(
        half == 0, jnp.concatenate([kept, taken], 0), jnp.concatenate([taken, kept], 0)
    )
    mask = lax.dynamic_slice_in_dim(typed_mask, half * cut, cut, 0)[None, :]
    mask_row = mask.astype(F32)

    residual = mask_row * scores
    residual_link = apply_link(residual)
    image = mask_row * residual_link + RIDGE * residual
    norm_now, curvature = dots((residual, residual), (residual, image))
    image_link = apply_link(image)
    direction, direction_link = residual, residual_link
    push, push_link = image, image_link
    step_size = norm_now / curvature
    solution = step_size * direction
    projected = step_size * direction_link
    for iteration in range(1, ITERS):
        residual = residual - step_size * push
        residual_link = residual_link - step_size * push_link
        image = mask_row * residual_link + RIDGE * residual
        norm_next, fresh, cross_a, cross_b, old, lean, size = dots(
            (residual, residual),
            (residual, image),
            (residual, push),
            (direction, image),
            (direction, push),
            (residual, direction),
            (direction, direction),
        )
        ratio = norm_next / norm_now
        curvature = fresh + ratio * (cross_a + cross_b) + ratio * ratio * old
        length = norm_next + ratio * (2.0 * lean) + ratio * ratio * size
        step_size = norm_next / jnp.maximum(curvature, 0.1 * RIDGE * length)
        if iteration + 1 < ITERS:
            image_link = apply_link(image)
            push_link = image_link + ratio * push_link
            push = image + ratio * push
        direction = residual + ratio * direction
        direction_link = residual_link + ratio * direction_link
        solution = solution + step_size * direction
        projected = projected + step_size * direction_link
        norm_now = norm_next
    imputed = jnp.where(mask == 1, scores, projected)

    both = jnp.stack([solution, imputed])
    traits = z_scores.shape[0]
    kept = lax.dynamic_slice_in_dim(both, half * traits, traits, 1)
    sent = lax.dynamic_slice_in_dim(both, (1 - half) * traits, traits, 1)
    whole = jnp.concatenate([kept, shift(sent, "xl", 1)], axis=2)
    whole = swap_halves(whole, half)
    return (whole[0], whole[1])


def solution(mesh):
    fine = Mesh(mesh.devices.reshape(SIZES), SAMPLE_AXES + BLOCK_AXES)
    placed = (P(SAMPLE_AXES, BLOCK_AXES), P(BLOCK_AXES), P(SAMPLE_AXES, BLOCK_AXES))
    return jax.shard_map(
        on_device,
        mesh=fine,
        in_specs=placed,
        out_specs=(P(SAMPLE_AXES, BLOCK_AXES), P(SAMPLE_AXES, BLOCK_AXES)),
        check_vma=False,
    )
```

```python
import jax
import jax.numpy as jnp
from jax import lax
from jax.sharding import Mesh, PartitionSpec as P

ITERS = 3
RIDGE = 0.1
EPSILON = 1e-05
BF16 = jnp.bfloat16
F32 = jnp.float32

SAMPLE_AXES = ("z", "y", "xl")
BLOCK_AXES = ("xh", "core")
PLANE_AXES = ("y", "xl")
SIZES = (8, 4, 2, 2, 2)
N_BLOCKS = 4


def shift(block, axis, distance):
    size = lax.axis_size(axis)
    return lax.ppermute(block, axis, [(i, (i + distance) % size) for i in range(size)])


def from_next(block):
    return lax.ppermute(block, BLOCK_AXES, [(i + 1, i) for i in range(N_BLOCKS - 1)])


def from_previous(block):
    return lax.ppermute(block, BLOCK_AXES, [(i, i + 1) for i in range(N_BLOCKS - 1)])


def contract_rows(first_mat, second_mat):
    return lax.dot_general(
        first_mat, second_mat, (((0,), (0,)), ((), ())), preferred_element_type=F32
    )


def rounded(values):
    return lax.reduce_precision(values, exponent_bits=8, mantissa_bits=7)


def split3(vector):
    high = rounded(vector)
    rest = vector - high
    mid = rounded(rest)
    return jnp.concatenate([high, mid, rest - mid], axis=0).astype(BF16)


def times(stacked, matrix, side):
    out = lax.dot_general(
        stacked, matrix, (((1,), (side,)), ((), ())), preferred_element_type=F32
    )
    rows = stacked.shape[0] // 3
    return out[2 * rows :] + out[rows : 2 * rows] + out[:rows]


def exchange(parts, axes):
    return lax.all_to_all(parts, axes, 0, 0, tiled=True)


def to_all(block, axes):
    copies = jnp.broadcast_to(block[None], (lax.axis_size(axes),) + block.shape)
    return exchange(lax.optimization_barrier(copies), axes)


def reduce_over(rows, axes):
    size = lax.axis_size(axes)
    parts = exchange(rows.reshape((size, -1) + rows.shape[1:]), axes)
    return jnp.sum(parts.astype(F32), axis=0)


def line_of(all_sums, all_squares, total_samples):
    coded_sum = jnp.sum(all_sums, axis=0, keepdims=True)
    mean_dosage = (coded_sum + total_samples) / total_samples
    squares = all_squares + 2.0 * coded_sum + total_samples
    variance = squares / total_samples - mean_dosage * mean_dosage
    scale = lax.rsqrt(variance + EPSILON)
    twos = 0.5 * (all_squares + coded_sum)
    zeros = 0.5 * (all_squares - coded_sum)
    ones = total_samples - all_squares
    level = rise = spread = 0.0
    for dosage, count in ((0.0, zeros), (1.0, ones), (2.0, twos)):
        away = dosage - mean_dosage
        value = rounded(away * scale)
        level = level + count * value
        rise = rise + count * value * away
        spread = spread + count * away * away
    slope = jnp.where(spread > 0.0, rise / jnp.where(spread > 0.0, spread, 1.0), scale)
    return level / total_samples, slope


def on_device(genotypes, typed_mask, z_scores):
    samples_dev, width = genotypes.shape
    total_samples = samples_dev * lax.axis_size(SAMPLE_AXES)
    coded = lax.optimization_barrier((genotypes - 1).astype(BF16))
    following = from_next(coded)

    def column_sums(values):
        return jnp.sum(values.astype(F32), axis=0, keepdims=True)

    def centred(row_sums, others, other_sums):
        counts = contract_rows(coded, others)
        return (counts - row_sums[0][:, None] * (other_sums / samples_dev)).astype(BF16)

    sums = column_sums(coded)
    squares = column_sums(coded * coded)
    own_part = centred(sums, coded, sums)
    own_sum = lax.psum_scatter(own_part, "z", scatter_dimension=0, tiled=True)

    local = jnp.concatenate([sums, squares], axis=0)
    local, own_part = lax.optimization_barrier((local, own_part))
    everyone = to_all(local, SAMPLE_AXES)
    statistics = jnp.concatenate(
        [everyone[:, 0], jnp.sum(everyone[:, 1], axis=0, keepdims=True)], axis=0
    )
    statistics, following = lax.optimization_barrier((statistics, following))
    next_statistics = from_next(statistics)

    edge_part = centred(sums, following, column_sums(following))
    edge_sum = reduce_over(edge_part, PLANE_AXES).astype(BF16)
    edge_sum, own_sum = lax.optimization_barrier((edge_sum, own_sum))
    edge_sum = lax.psum_scatter(edge_sum, "z", scatter_dimension=0, tiled=True).astype(F32)
    own_sum = reduce_over(own_sum, PLANE_AXES)

    def lines(table):
        level, slope = line_of(table[:-1], table[-1:], total_samples)
        off = (table[:-1] - jnp.mean(table[:-1], axis=0, keepdims=True)) * slope
        return level, slope, off

    row_lines = lines(statistics)
    rows = own_sum.shape[0]
    place, plane = lax.axis_index("z"), lax.axis_index(PLANE_AXES)
    n_place, n_plane = lax.axis_size("z"), lax.axis_size(PLANE_AXES)

    def link_rows(within, first_row, column_lines):
        level, slope, off = column_lines
        level_rows, slope_rows, off_rows = [
            lax.dynamic_slice_in_dim(values, first_row, rows, axis=1) for values in row_lines
        ]
        between = lax.dot_general(
            off_rows,
            off,
            (((0,), (0,)), ((), ())),
            precision=lax.Precision.HIGHEST,
            preferred_element_type=F32,
        )
        link = within * slope * slope_rows[0][:, None] + between / samples_dev
        return (link / total_samples + level_rows[0][:, None] * level).astype(BF16)

    own_rows = link_rows(own_sum, (place * n_plane + plane) * rows, row_lines)
    edge_rows = link_rows(edge_sum, (plane * n_place + place) * rows, lines(next_statistics))
    own = to_all(own_rows, PLANE_AXES).reshape(-1, width)
    own = lax.all_gather(own, "z", axis=0, tiled=True)
    edge = to_all(edge_rows, "z").reshape(-1, width)
    edge = to_all(edge, PLANE_AXES).reshape(-1, width)

    def apply_link(vector):
        ahead = from_next(vector)
        mine = split3(vector)
        lower = from_previous(times(mine, edge, 0))
        result = times(mine, own, 1) + 0.5 * times(split3(ahead), edge, 1)
        return result + 0.5 * lower

    def dots(*pairs):
        local = jnp.stack([jnp.sum(a * b, axis=1) for a, b in pairs])
        local = local + shift(local, "core", 1)
        return (local + shift(local, "xh", 1))[:, :, None]

    mask = typed_mask[None, :]
    mask_row = mask.astype(F32)
    scores = z_scores

    residual = mask_row * scores
    residual_link = apply_link(residual)
    image = mask_row * residual_link + RIDGE * residual
    norm_now, curvature = dots((residual, residual), (residual, image))
    image_link = apply_link(image)
    direction, direction_link = residual, residual_link
    push, push_link = image, image_link
    step_size = norm_now / curvature
    solution = step_size * direction
    projected = step_size * direction_link
    for iteration in range(1, ITERS):
        residual = residual - step_size * push
        residual_link = residual_link - step_size * push_link
        image = mask_row * residual_link + RIDGE * residual
        norm_next, fresh, cross_a, cross_b, old, lean, size = dots(
            (residual, residual),
            (residual, image),
            (residual, push),
            (direction, image),
            (direction, push),
            (residual, direction),
            (direction, direction),
        )
        ratio = norm_next / norm_now
        curvature = fresh + ratio * (cross_a + cross_b) + ratio * ratio * old
        length = norm_next + ratio * (2.0 * lean) + ratio * ratio * size
        step_size = norm_next / jnp.maximum(curvature, 0.1 * RIDGE * length)
        if iteration + 1 < ITERS:
            image_link = apply_link(image)
            push_link = image_link + ratio * push_link
            push = image + ratio * push
        direction = residual + ratio * direction
        direction_link = residual_link + ratio * direction_link
        solution = solution + step_size * direction
        projected = projected + step_size * direction_link
        norm_now = norm_next
    imputed = jnp.where(mask == 1, scores, projected)

    return (solution, imputed)


def solution(mesh):
    fine = Mesh(mesh.devices.reshape(SIZES), SAMPLE_AXES + BLOCK_AXES)
    placed = (P(SAMPLE_AXES, BLOCK_AXES), P(BLOCK_AXES), P(SAMPLE_AXES, BLOCK_AXES))
    return jax.shard_map(
        on_device,
        mesh=fine,
        in_specs=placed,
        out_specs=(P(SAMPLE_AXES, BLOCK_AXES), P(SAMPLE_AXES, BLOCK_AXES)),
        check_vma=False,
    )
```

```python
import jax
import jax.numpy as jnp
from jax import lax
from jax.sharding import Mesh, PartitionSpec as P

ITERS = 3
RIDGE = 0.1
EPSILON = 1e-05
BF16 = jnp.bfloat16
F32 = jnp.float32

SAMPLE_AXES = ("z", "y", "xl")
BLOCK_AXES = ("xh", "core")
PLANE_AXES = ("y", "xl")
FLAT_AXES = ("z", "xl")
SIZES = (8, 4, 2, 2, 2)
N_BLOCKS = 4


def shift(block, axis, distance):
    size = lax.axis_size(axis)
    return lax.ppermute(block, axis, [(i, (i + distance) % size) for i in range(size)])


def from_next(block):
    return lax.ppermute(block, BLOCK_AXES, [(i + 1, i) for i in range(N_BLOCKS - 1)])


def from_previous(block):
    return lax.ppermute(block, BLOCK_AXES, [(i, i + 1) for i in range(N_BLOCKS - 1)])


def contract_rows(first_mat, second_mat):
    return lax.dot_general(
        first_mat, second_mat, (((0,), (0,)), ((), ())), preferred_element_type=F32
    )


def rounded(values):
    return lax.reduce_precision(values, exponent_bits=8, mantissa_bits=7)


def split3(vector):
    high = rounded(vector)
    rest = vector - high
    mid = rounded(rest)
    return jnp.concatenate([high, mid, rest - mid], axis=0).astype(BF16)


def times(stacked, matrix, side):
    out = lax.dot_general(
        stacked, matrix, (((1,), (side,)), ((), ())), preferred_element_type=F32
    )
    rows = stacked.shape[0] // 3
    return out[2 * rows :] + out[rows : 2 * rows] + out[:rows]


def exchange(parts, axes):
    return lax.all_to_all(parts, axes, 0, 0, tiled=True)


def to_all(block, axes):
    copies = jnp.broadcast_to(block[None], (lax.axis_size(axes),) + block.shape)
    return exchange(lax.optimization_barrier(copies), axes)


def reduce_over(rows, axes):
    size = lax.axis_size(axes)
    parts = exchange(rows.reshape((size, -1) + rows.shape[1:]), axes)
    return jnp.sum(parts.astype(F32), axis=0)


def line_of(all_sums, all_squares, total_samples):
    coded_sum = jnp.sum(all_sums, axis=0, keepdims=True)
    mean_dosage = (coded_sum + total_samples) / total_samples
    squares = all_squares + 2.0 * coded_sum + total_samples
    variance = squares / total_samples - mean_dosage * mean_dosage
    scale = lax.rsqrt(variance + EPSILON)
    twos = 0.5 * (all_squares + coded_sum)
    zeros = 0.5 * (all_squares - coded_sum)
    ones = total_samples - all_squares
    level = rise = spread = 0.0
    for dosage, count in ((0.0, zeros), (1.0, ones), (2.0, twos)):
        away = dosage - mean_dosage
        value = rounded(away * scale)
        level = level + count * value
        rise = rise + count * value * away
        spread = spread + count * away * away
    slope = jnp.where(spread > 0.0, rise / jnp.where(spread > 0.0, spread, 1.0), scale)
    return level / total_samples, slope


def on_device(genotypes, typed_mask, z_scores):
    samples_dev, width = genotypes.shape
    total_samples = samples_dev * lax.axis_size(SAMPLE_AXES)
    cut = width // 2
    coded = lax.optimization_barrier((genotypes - 1).astype(BF16))
    following = [from_next(coded[:, :cut]), from_next(coded[:, cut:])]

    def column_sums(values):
        return jnp.sum(values.astype(F32), axis=0, keepdims=True)

    def centred(row_sums, others, other_sums):
        counts = contract_rows(coded, others)
        return (counts - row_sums[0][:, None] * (other_sums / samples_dev)).astype(BF16)

    sums = column_sums(coded)
    squares = column_sums(coded * coded)
    own_part = centred(sums, coded, sums)
    own_sum = lax.psum_scatter(own_part, "z", scatter_dimension=0, tiled=True)

    everyone = to_all(jnp.concatenate([sums, squares], axis=0), SAMPLE_AXES)
    statistics = jnp.concatenate(
        [everyone[:, 0], jnp.sum(everyone[:, 1], axis=0, keepdims=True)], axis=0
    )
    next_statistics = from_next(statistics)

    edge_sum = [
        reduce_over(centred(sums, piece, column_sums(piece)), "y").astype(BF16)
        for piece in following
    ]
    edge_sum, own_sum = lax.optimization_barrier((edge_sum, own_sum))
    edge_sum = reduce_over(jnp.concatenate(edge_sum, axis=1), FLAT_AXES)
    own_sum = reduce_over(own_sum, PLANE_AXES)

    def lines(table):
        level, slope = line_of(table[:-1], table[-1:], total_samples)
        off = (table[:-1] - jnp.mean(table[:-1], axis=0, keepdims=True)) * slope
        return level, slope, off

    row_lines = lines(statistics)
    rows = own_sum.shape[0]
    own_place = lax.axis_index("z") * lax.axis_size(PLANE_AXES) + lax.axis_index(PLANE_AXES)
    edge_place = lax.axis_index("y") * lax.axis_size(FLAT_AXES) + lax.axis_index(FLAT_AXES)

    def link_rows(within, first_row, column_lines):
        level, slope, off = column_lines
        level_rows, slope_rows, off_rows = [
            lax.dynamic_slice_in_dim(values, first_row, rows, axis=1) for values in row_lines
        ]
        between = lax.dot_general(
            off_rows,
            off,
            (((0,), (0,)), ((), ())),
            precision=lax.Precision.HIGHEST,
            preferred_element_type=F32,
        )
        link = within * slope * slope_rows[0][:, None] + between / samples_dev
        return (link / total_samples + level_rows[0][:, None] * level).astype(BF16)

    own_rows = link_rows(own_sum, own_place * rows, row_lines)
    edge_rows = link_rows(edge_sum, edge_place * rows, lines(next_statistics))
    own = to_all(own_rows, PLANE_AXES).reshape(-1, width)
    own = lax.all_gather(own, "z", axis=0, tiled=True)
    edge = to_all(edge_rows, FLAT_AXES).reshape(-1, width)
    edge = to_all(edge, "y").reshape(-1, width)

    def apply_link(vector):
        ahead = from_next(vector)
        mine = split3(vector)
        lower = from_previous(times(mine, edge, 0))
        result = times(mine, own, 1) + 0.5 * times(split3(ahead), edge, 1)
        return result + 0.5 * lower

    def dots(*pairs):
        local = jnp.stack([jnp.sum(a * b, axis=1) for a, b in pairs])
        local = local + shift(local, "core", 1)
        return (local + shift(local, "xh", 1))[:, :, None]

    mask = typed_mask[None, :]
    mask_row = mask.astype(F32)
    scores = z_scores

    residual = mask_row * scores
    residual_link = apply_link(residual)
    image = mask_row * residual_link + RIDGE * residual
    norm_now, curvature = dots((residual, residual), (residual, image))
    image_link = apply_link(image)
    direction, direction_link = residual, residual_link
    push, push_link = image, image_link
    step_size = norm_now / curvature
    solution = step_size * direction
    projected = step_size * direction_link
    for iteration in range(1, ITERS):
        residual = residual - step_size * push
        residual_link = residual_link - step_size * push_link
        image = mask_row * residual_link + RIDGE * residual
        norm_next, fresh, cross_a, cross_b, old, lean, size = dots(
            (residual, residual),
            (residual, image),
            (residual, push),
            (direction, image),
            (direction, push),
            (residual, direction),
            (direction, direction),
        )
        ratio = norm_next / norm_now
        curvature = fresh + ratio * (cross_a + cross_b) + ratio * ratio * old
        length = norm_next + ratio * (2.0 * lean) + ratio * ratio * size
        step_size = norm_next / jnp.maximum(curvature, 0.1 * RIDGE * length)
        if iteration + 1 < ITERS:
            image_link = apply_link(image)
            push_link = image_link + ratio * push_link
            push = image + ratio * push
        direction = residual + ratio * direction
        direction_link = residual_link + ratio * direction_link
        solution = solution + step_size * direction
        projected = projected + step_size * direction_link
        norm_now = norm_next
    imputed = jnp.where(mask == 1, scores, projected)

    return (solution, imputed)


def solution(mesh):
    fine = Mesh(mesh.devices.reshape(SIZES), SAMPLE_AXES + BLOCK_AXES)
    placed = (P(SAMPLE_AXES, BLOCK_AXES), P(BLOCK_AXES), P(SAMPLE_AXES, BLOCK_AXES))
    return jax.shard_map(
        on_device,
        mesh=fine,
        in_specs=placed,
        out_specs=(P(SAMPLE_AXES, BLOCK_AXES), P(SAMPLE_AXES, BLOCK_AXES)),
        check_vma=False,
    )
```

```python
import jax
import jax.numpy as jnp
from jax import lax
from jax.sharding import Mesh, PartitionSpec as P

ITERS = 3
RIDGE = 0.1
EPSILON = 1e-05
BF16 = jnp.bfloat16
F32 = jnp.float32

SAMPLE_AXES = ("z", "y", "xl")
BLOCK_AXES = ("xh", "core")
PLANE_AXES = ("y", "xl")
SIZES = (8, 4, 2, 2, 2)
N_BLOCKS = 4


def shift(block, axis, distance):
    size = lax.axis_size(axis)
    return lax.ppermute(block, axis, [(i, (i + distance) % size) for i in range(size)])


def from_next(block):
    return lax.ppermute(block, BLOCK_AXES, [(i + 1, i) for i in range(N_BLOCKS - 1)])


def from_previous(block):
    return lax.ppermute(block, BLOCK_AXES, [(i, i + 1) for i in range(N_BLOCKS - 1)])


def contract_rows(first_mat, second_mat):
    return lax.dot_general(
        first_mat, second_mat, (((0,), (0,)), ((), ())), preferred_element_type=F32
    )


def rounded(values):
    return lax.reduce_precision(values, exponent_bits=8, mantissa_bits=7)


def split3(vector):
    high = rounded(vector)
    rest = vector - high
    mid = rounded(rest)
    return jnp.concatenate([high, mid, rest - mid], axis=0).astype(BF16)


def times(stacked, matrix, side):
    out = lax.dot_general(
        stacked, matrix, (((1,), (side,)), ((), ())), preferred_element_type=F32
    )
    rows = stacked.shape[0] // 3
    return out[2 * rows :] + out[rows : 2 * rows] + out[:rows]


def exchange(parts, axes):
    return lax.all_to_all(parts, axes, 0, 0, tiled=True)


def to_all(block, axes):
    copies = jnp.broadcast_to(block[None], (lax.axis_size(axes),) + block.shape)
    return exchange(lax.optimization_barrier(copies), axes)


def reduce_over(rows, axes):
    size = lax.axis_size(axes)
    parts = exchange(rows.reshape((size, -1) + rows.shape[1:]), axes)
    return jnp.sum(parts.astype(F32), axis=0)


def line_of(all_sums, all_squares, total_samples):
    coded_sum = jnp.sum(all_sums, axis=0, keepdims=True)
    mean_dosage = (coded_sum + total_samples) / total_samples
    squares = all_squares + 2.0 * coded_sum + total_samples
    variance = squares / total_samples - mean_dosage * mean_dosage
    scale = lax.rsqrt(variance + EPSILON)
    twos = 0.5 * (all_squares + coded_sum)
    zeros = 0.5 * (all_squares - coded_sum)
    ones = total_samples - all_squares
    level = rise = spread = 0.0
    for dosage, count in ((0.0, zeros), (1.0, ones), (2.0, twos)):
        away = dosage - mean_dosage
        value = rounded(away * scale)
        level = level + count * value
        rise = rise + count * value * away
        spread = spread + count * away * away
    slope = jnp.where(spread > 0.0, rise / jnp.where(spread > 0.0, spread, 1.0), scale)
    return level / total_samples, slope


def on_device(genotypes, typed_mask, z_scores):
    samples_dev, width = genotypes.shape
    total_samples = samples_dev * lax.axis_size(SAMPLE_AXES)
    coded = lax.optimization_barrier((genotypes - 1).astype(BF16))
    following = from_next(coded)

    def column_sums(values):
        return jnp.sum(values.astype(F32), axis=0, keepdims=True)

    def centred(row_sums, others, other_sums):
        counts = contract_rows(coded, others)
        return (counts - row_sums[0][:, None] * (other_sums / samples_dev)).astype(BF16)

    sums = column_sums(coded)
    squares = column_sums(coded * coded)
    following_sums = from_next(sums)
    own_part = centred(sums, coded, sums)
    own_sum = lax.psum_scatter(own_part, "z", scatter_dimension=0, tiled=True)

    everyone = to_all(jnp.concatenate([sums, squares], axis=0), ("z", "y"))
    table = jnp.concatenate(
        [everyone[:, 0], jnp.sum(everyone[:, 1], axis=0, keepdims=True)], axis=0
    )
    table, following = lax.optimization_barrier((table, following))
    partner = shift(table, "xl", 1)
    statistics = jnp.concatenate([table[:-1], partner[:-1], table[-1:] + partner[-1:]], axis=0)
    next_statistics = from_next(statistics)

    edge_part = centred(sums, following, following_sums)
    edge_sum = reduce_over(edge_part, PLANE_AXES).astype(BF16)
    edge_sum, own_sum = lax.optimization_barrier((edge_sum, own_sum))
    own_sum = reduce_over(own_sum, PLANE_AXES)
    edge_sum = reduce_over(edge_sum, "z")

    def lines(table):
        level, slope = line_of(table[:-1], table[-1:], total_samples)
        off = (table[:-1] - jnp.mean(table[:-1], axis=0, keepdims=True)) * slope
        return level, slope, off

    row_lines = lines(statistics)
    rows = own_sum.shape[0]
    place, plane = lax.axis_index("z"), lax.axis_index(PLANE_AXES)
    n_place, n_plane = lax.axis_size("z"), lax.axis_size(PLANE_AXES)

    def link_rows(within, first_row, column_lines):
        level, slope, off = column_lines
        level_rows, slope_rows, off_rows = [
            lax.dynamic_slice_in_dim(values, first_row, rows, axis=1) for values in row_lines
        ]
        between = lax.dot_general(
            off_rows,
            off,
            (((0,), (0,)), ((), ())),
            precision=lax.Precision.HIGHEST,
            preferred_element_type=F32,
        )
        link = within * slope * slope_rows[0][:, None] + between / samples_dev
        return (link / total_samples + level_rows[0][:, None] * level).astype(BF16)

    own_rows = link_rows(own_sum, (place * n_plane + plane) * rows, row_lines)
    edge_rows = link_rows(edge_sum, (plane * n_place + place) * rows, lines(next_statistics))
    own = to_all(own_rows, PLANE_AXES).reshape(-1, width)
    own = lax.all_gather(own, "z", axis=0, tiled=True)
    edge = to_all(edge_rows, "z").reshape(-1, width)
    edge = to_all(edge, PLANE_AXES).reshape(-1, width)

    def apply_link(vector):
        ahead = from_next(vector)
        mine = split3(vector)
        lower = from_previous(times(mine, edge, 0))
        result = times(mine, own, 1) + 0.5 * times(split3(ahead), edge, 1)
        return result + 0.5 * lower

    def dots(*pairs):
        local = jnp.stack([jnp.sum(a * b, axis=1) for a, b in pairs])
        local = local + shift(local, "core", 1)
        return (local + shift(local, "xh", 1))[:, :, None]

    mask = typed_mask[None, :]
    mask_row = mask.astype(F32)
    scores = z_scores

    residual = mask_row * scores
    residual_link = apply_link(residual)
    image = mask_row * residual_link + RIDGE * residual
    norm_now, curvature = dots((residual, residual), (residual, image))
    image_link = apply_link(image)
    direction, direction_link = residual, residual_link
    push, push_link = image, image_link
    step_size = norm_now / curvature
    solution = step_size * direction
    projected = step_size * direction_link
    for iteration in range(1, ITERS):
        residual = residual - step_size * push
        residual_link = residual_link - step_size * push_link
        image = mask_row * residual_link + RIDGE * residual
        norm_next, fresh, cross_a, cross_b, old, lean, size = dots(
            (residual, residual),
            (residual, image),
            (residual, push),
            (direction, image),
            (direction, push),
            (residual, direction),
            (direction, direction),
        )
        ratio = norm_next / norm_now
        curvature = fresh + ratio * (cross_a + cross_b) + ratio * ratio * old
        length = norm_next + ratio * (2.0 * lean) + ratio * ratio * size
        step_size = norm_next / jnp.maximum(curvature, 0.1 * RIDGE * length)
        if iteration + 1 < ITERS:
            image_link = apply_link(image)
            push_link = image_link + ratio * push_link
            push = image + ratio * push
        direction = residual + ratio * direction
        direction_link = residual_link + ratio * direction_link
        solution = solution + step_size * direction
        projected = projected + step_size * direction_link
        norm_now = norm_next
    imputed = jnp.where(mask == 1, scores, projected)

    return (solution, imputed)


def solution(mesh):
    fine = Mesh(mesh.devices.reshape(SIZES), SAMPLE_AXES + BLOCK_AXES)
    placed = (P(SAMPLE_AXES, BLOCK_AXES), P(BLOCK_AXES), P(SAMPLE_AXES, BLOCK_AXES))
    return jax.shard_map(
        on_device,
        mesh=fine,
        in_specs=placed,
        out_specs=(P(SAMPLE_AXES, BLOCK_AXES), P(SAMPLE_AXES, BLOCK_AXES)),
        check_vma=False,
    )
```

```python
import jax
import jax.numpy as jnp
from jax import lax
from jax.sharding import Mesh, PartitionSpec as P

ITERS = 3
RIDGE = 0.1
EPSILON = 1e-05
BF16 = jnp.bfloat16
F32 = jnp.float32

SAMPLE_AXES = ("z", "y", "xl")
BLOCK_AXES = ("xh", "core")
PLANE_AXES = ("y", "xl")
SIZES = (8, 4, 2, 2, 2)
N_BLOCKS = 4


def shift(block, axis, distance):
    size = lax.axis_size(axis)
    return lax.ppermute(block, axis, [(i, (i + distance) % size) for i in range(size)])


def from_next(block):
    return lax.ppermute(block, BLOCK_AXES, [(i + 1, i) for i in range(N_BLOCKS - 1)])


def from_previous(block):
    return lax.ppermute(block, BLOCK_AXES, [(i, i + 1) for i in range(N_BLOCKS - 1)])


def contract_rows(first_mat, second_mat):
    return lax.dot_general(
        first_mat, second_mat, (((0,), (0,)), ((), ())), preferred_element_type=F32
    )


def rounded(values):
    return lax.reduce_precision(values, exponent_bits=8, mantissa_bits=7)


def split3(vector):
    high = rounded(vector)
    rest = vector - high
    mid = rounded(rest)
    return jnp.concatenate([high, mid, rest - mid], axis=0).astype(BF16)


def times(stacked, matrix, side):
    out = lax.dot_general(
        stacked, matrix, (((1,), (side,)), ((), ())), preferred_element_type=F32
    )
    rows = stacked.shape[0] // 3
    return out[2 * rows :] + out[rows : 2 * rows] + out[:rows]


def exchange(parts, axes):
    return lax.all_to_all(parts, axes, 0, 0, tiled=True)


def to_all(block, axes):
    copies = jnp.broadcast_to(block[None], (lax.axis_size(axes),) + block.shape)
    return exchange(lax.optimization_barrier(copies), axes)


def reduce_over(rows, axes):
    size = lax.axis_size(axes)
    parts = exchange(rows.reshape((size, -1) + rows.shape[1:]), axes)
    return jnp.sum(parts.astype(F32), axis=0)


def line_of(all_sums, all_squares, total_samples):
    coded_sum = jnp.sum(all_sums, axis=0, keepdims=True)
    mean_dosage = (coded_sum + total_samples) / total_samples
    squares = all_squares + 2.0 * coded_sum + total_samples
    variance = squares / total_samples - mean_dosage * mean_dosage
    scale = lax.rsqrt(variance + EPSILON)
    twos = 0.5 * (all_squares + coded_sum)
    zeros = 0.5 * (all_squares - coded_sum)
    ones = total_samples - all_squares
    level = rise = spread = 0.0
    for dosage, count in ((0.0, zeros), (1.0, ones), (2.0, twos)):
        away = dosage - mean_dosage
        value = rounded(away * scale)
        level = level + count * value
        rise = rise + count * value * away
        spread = spread + count * away * away
    slope = jnp.where(spread > 0.0, rise / jnp.where(spread > 0.0, spread, 1.0), scale)
    return level / total_samples, slope


def on_device(genotypes, typed_mask, z_scores):
    samples_dev, width = genotypes.shape
    total_samples = samples_dev * lax.axis_size(SAMPLE_AXES)
    coded = lax.optimization_barrier((genotypes - 1).astype(BF16))
    following = from_next(coded)

    def column_sums(values):
        return jnp.sum(values.astype(F32), axis=0, keepdims=True)

    def centred(row_sums, others, other_sums):
        counts = contract_rows(coded, others)
        return (counts - row_sums[0][:, None] * (other_sums / samples_dev)).astype(BF16)

    sums = column_sums(coded)
    squares = column_sums(coded * coded)
    following_sums = from_next(sums)
    own_part = centred(sums, coded, sums)
    own_sum = lax.psum_scatter(own_part, "z", scatter_dimension=0, tiled=True)

    everyone = to_all(jnp.concatenate([sums, squares], axis=0), ("z", "y"))
    table = jnp.concatenate(
        [everyone[:, 0], jnp.sum(everyone[:, 1], axis=0, keepdims=True)], axis=0
    )
    table, following = lax.optimization_barrier((table, following))
    partner = shift(table, "xl", 1)
    statistics = jnp.concatenate([table[:-1], partner[:-1], table[-1:] + partner[-1:]], axis=0)
    next_statistics = from_next(statistics)

    edge_part = centred(sums, following, following_sums)
    edge_sum = reduce_over(edge_part, "y").astype(BF16)
    edge_sum, own_sum = lax.optimization_barrier((edge_sum, own_sum))
    n_place = lax.axis_size("z")
    edge_sum = edge_sum.reshape(2, n_place, -1, width).swapaxes(0, 1).reshape(-1, width)
    edge_sum = lax.psum_scatter(edge_sum, "z", scatter_dimension=0, tiled=True)
    edge_sum = edge_sum.reshape(2, -1, width)
    side = lax.axis_index("xl").astype(jnp.uint32)
    kept = lax.dynamic_index_in_dim(edge_sum, side, 0, keepdims=False)
    sent = lax.dynamic_index_in_dim(edge_sum, 1 - side, 0, keepdims=False)
    edge_sum = kept.astype(F32) + shift(sent, "xl", 1).astype(F32)
    own_sum = reduce_over(own_sum, PLANE_AXES)

    def lines(table):
        level, slope = line_of(table[:-1], table[-1:], total_samples)
        off = (table[:-1] - jnp.mean(table[:-1], axis=0, keepdims=True)) * slope
        return level, slope, off

    row_lines = lines(statistics)
    rows = own_sum.shape[0]
    place, plane = lax.axis_index("z"), lax.axis_index(PLANE_AXES)
    n_plane = lax.axis_size(PLANE_AXES)

    def link_rows(within, first_row, column_lines):
        level, slope, off = column_lines
        level_rows, slope_rows, off_rows = [
            lax.dynamic_slice_in_dim(values, first_row, rows, axis=1) for values in row_lines
        ]
        between = lax.dot_general(
            off_rows,
            off,
            (((0,), (0,)), ((), ())),
            precision=lax.Precision.HIGHEST,
            preferred_element_type=F32,
        )
        link = within * slope * slope_rows[0][:, None] + between / samples_dev
        return (link / total_samples + level_rows[0][:, None] * level).astype(BF16)

    own_rows = link_rows(own_sum, (place * n_plane + plane) * rows, row_lines)
    edge_rows = link_rows(edge_sum, (plane * n_place + place) * rows, lines(next_statistics))
    own = to_all(own_rows, PLANE_AXES).reshape(-1, width)
    own = lax.all_gather(own, "z", axis=0, tiled=True)
    edge = to_all(edge_rows, "z").reshape(-1, width)
    edge = to_all(edge, PLANE_AXES).reshape(-1, width)

    def apply_link(vector):
        ahead = from_next(vector)
        mine = split3(vector)
        lower = from_previous(times(mine, edge, 0))
        result = times(mine, own, 1) + 0.5 * times(split3(ahead), edge, 1)
        return result + 0.5 * lower

    def dots(*pairs):
        local = jnp.stack([jnp.sum(a * b, axis=1) for a, b in pairs])
        local = local + shift(local, "core", 1)
        return (local + shift(local, "xh", 1))[:, :, None]

    mask = typed_mask[None, :]
    mask_row = mask.astype(F32)
    scores = z_scores

    residual = mask_row * scores
    residual_link = apply_link(residual)
    image = mask_row * residual_link + RIDGE * residual
    norm_now, curvature = dots((residual, residual), (residual, image))
    image_link = apply_link(image)
    direction, direction_link = residual, residual_link
    push, push_link = image, image_link
    step_size = norm_now / curvature
    solution = step_size * direction
    projected = step_size * direction_link
    for iteration in range(1, ITERS):
        residual = residual - step_size * push
        residual_link = residual_link - step_size * push_link
        image = mask_row * residual_link + RIDGE * residual
        norm_next, fresh, cross_a, cross_b, old, lean, size = dots(
            (residual, residual),
            (residual, image),
            (residual, push),
            (direction, image),
            (direction, push),
            (residual, direction),
            (direction, direction),
        )
        ratio = norm_next / norm_now
        curvature = fresh + ratio * (cross_a + cross_b) + ratio * ratio * old
        length = norm_next + ratio * (2.0 * lean) + ratio * ratio * size
        step_size = norm_next / jnp.maximum(curvature, 0.1 * RIDGE * length)
        if iteration + 1 < ITERS:
            image_link = apply_link(image)
            push_link = image_link + ratio * push_link
            push = image + ratio * push
        direction = residual + ratio * direction
        direction_link = residual_link + ratio * direction_link
        solution = solution + step_size * direction
        projected = projected + step_size * direction_link
        norm_now = norm_next
    imputed = jnp.where(mask == 1, scores, projected)

    return (solution, imputed)


def solution(mesh):
    fine = Mesh(mesh.devices.reshape(SIZES), SAMPLE_AXES + BLOCK_AXES)
    placed = (P(SAMPLE_AXES, BLOCK_AXES), P(BLOCK_AXES), P(SAMPLE_AXES, BLOCK_AXES))
    return jax.shard_map(
        on_device,
        mesh=fine,
        in_specs=placed,
        out_specs=(P(SAMPLE_AXES, BLOCK_AXES), P(SAMPLE_AXES, BLOCK_AXES)),
        check_vma=False,
    )
```

```python
import jax
import jax.numpy as jnp
from jax import lax
from jax.sharding import Mesh, PartitionSpec as P

ITERS = 3
RIDGE = 0.1
EPSILON = 1e-05
BF16 = jnp.bfloat16
F32 = jnp.float32

SAMPLE_AXES = ("z", "y", "xl")
BLOCK_AXES = ("xh", "core")
PLANE_AXES = ("y", "xl")
SIZES = (8, 4, 2, 2, 2)
N_BLOCKS = 4


def shift(block, axis, distance):
    size = lax.axis_size(axis)
    return lax.ppermute(block, axis, [(i, (i + distance) % size) for i in range(size)])


def from_next(block):
    return lax.ppermute(block, BLOCK_AXES, [(i + 1, i) for i in range(N_BLOCKS - 1)])


def from_previous(block):
    return lax.ppermute(block, BLOCK_AXES, [(i, i + 1) for i in range(N_BLOCKS - 1)])


def contract_rows(first_mat, second_mat):
    return lax.dot_general(
        first_mat, second_mat, (((0,), (0,)), ((), ())), preferred_element_type=F32
    )


def rounded(values):
    return lax.reduce_precision(values, exponent_bits=8, mantissa_bits=7)


def split3(vector):
    high = rounded(vector)
    rest = vector - high
    mid = rounded(rest)
    return jnp.concatenate([high, mid, rest - mid], axis=0).astype(BF16)


def times(stacked, matrix, side):
    out = lax.dot_general(
        stacked, matrix, (((1,), (side,)), ((), ())), preferred_element_type=F32
    )
    rows = stacked.shape[0] // 3
    return out[2 * rows :] + out[rows : 2 * rows] + out[:rows]


def add(first, second):
    return (first.astype(F32) + second.astype(F32)).astype(BF16)


def ring_reduce(parts, axis):
    size = lax.axis_size(axis)
    half = size // 2
    here = lax.axis_index(axis).astype(jnp.uint32)

    def part(offset):
        return lax.dynamic_index_in_dim(parts, (here + (offset + size)) & (size - 1), 1, keepdims=False)

    far = part(half)
    right, left = shift(far[:1], axis, 1), shift(far[1:], axis, -1)
    for offset in range(half - 1, 0, -1):
        ahead, behind = part(offset), part(-offset)
        if offset == half - 1:
            ahead = jnp.concatenate([add(ahead[:1], right), ahead[1:]], axis=0)
            behind = jnp.concatenate([behind[:1], add(behind[1:], left)], axis=0)
        else:
            ahead, behind = add(ahead, right), add(behind, left)
        right, left = shift(ahead, axis, 1), shift(behind, axis, -1)
    mine = part(0).astype(F32)
    if half == 1:
        return mine + jnp.concatenate([right, left], axis=0).astype(F32)
    return mine + right.astype(F32) + left.astype(F32)


def exchange(parts, axes):
    return lax.all_to_all(parts, axes, 0, 0, tiled=True)


def to_all(block, axes):
    copies = jnp.broadcast_to(block[None], (lax.axis_size(axes),) + block.shape)
    return exchange(lax.optimization_barrier(copies), axes)


def reduce_over(rows, axes):
    size = lax.axis_size(axes)
    parts = exchange(rows.reshape((size, -1) + rows.shape[1:]), axes)
    return jnp.sum(parts.astype(F32), axis=0)


def line_of(all_sums, all_squares, total_samples):
    coded_sum = jnp.sum(all_sums, axis=0, keepdims=True)
    mean_dosage = (coded_sum + total_samples) / total_samples
    squares = all_squares + 2.0 * coded_sum + total_samples
    variance = squares / total_samples - mean_dosage * mean_dosage
    scale = lax.rsqrt(variance + EPSILON)
    twos = 0.5 * (all_squares + coded_sum)
    zeros = 0.5 * (all_squares - coded_sum)
    ones = total_samples - all_squares
    level = rise = spread = 0.0
    for dosage, count in ((0.0, zeros), (1.0, ones), (2.0, twos)):
        away = dosage - mean_dosage
        value = rounded(away * scale)
        level = level + count * value
        rise = rise + count * value * away
        spread = spread + count * away * away
    slope = jnp.where(spread > 0.0, rise / jnp.where(spread > 0.0, spread, 1.0), scale)
    return level / total_samples, slope


def on_device(genotypes, typed_mask, z_scores):
    samples_dev, width = genotypes.shape
    total_samples = samples_dev * lax.axis_size(SAMPLE_AXES)
    coded = lax.optimization_barrier((genotypes - 1).astype(BF16))
    following = from_next(coded)

    def column_sums(values):
        return jnp.sum(values.astype(F32), axis=0, keepdims=True)

    def centred(row_sums, others, other_sums):
        counts = contract_rows(coded, others)
        return (counts - row_sums[0][:, None] * (other_sums / samples_dev)).astype(BF16)

    sums = column_sums(coded)
    squares = column_sums(coded * coded)
    following_sums = from_next(sums)
    own_part = centred(sums, coded, sums)
    own_sum = lax.psum_scatter(own_part, "z", scatter_dimension=0, tiled=True)

    everyone = to_all(jnp.concatenate([sums, squares], axis=0), ("z", "y"))
    table = jnp.concatenate(
        [everyone[:, 0], jnp.sum(everyone[:, 1], axis=0, keepdims=True)], axis=0
    )
    table, following = lax.optimization_barrier((table, following))
    partner = shift(table, "xl", 1)
    statistics = jnp.concatenate([table[:-1], partner[:-1], table[-1:] + partner[-1:]], axis=0)
    next_statistics = from_next(statistics)

    edge_part = centred(sums, following, following_sums)
    n_place, n_row = lax.axis_size("z"), lax.axis_size("y")
    edge_part = edge_part.reshape(n_row, 2, -1, width).swapaxes(0, 1)
    edge_sum = ring_reduce(edge_part, "y").astype(BF16)
    edge_sum, own_sum = lax.optimization_barrier((edge_sum, own_sum))
    edge_sum = edge_sum.reshape(2, n_place, -1, width).swapaxes(0, 1).reshape(-1, width)
    edge_sum = lax.psum_scatter(edge_sum, "z", scatter_dimension=0, tiled=True)
    edge_sum = edge_sum.reshape(2, -1, width)
    side = lax.axis_index("xl").astype(jnp.uint32)
    kept = lax.dynamic_index_in_dim(edge_sum, side, 0, keepdims=False)
    sent = lax.dynamic_index_in_dim(edge_sum, 1 - side, 0, keepdims=False)
    edge_sum = kept.astype(F32) + shift(sent, "xl", 1).astype(F32)
    own_sum = reduce_over(own_sum, PLANE_AXES)

    def lines(table):
        level, slope = line_of(table[:-1], table[-1:], total_samples)
        off = (table[:-1] - jnp.mean(table[:-1], axis=0, keepdims=True)) * slope
        return level, slope, off

    row_lines = lines(statistics)
    rows = own_sum.shape[0]
    place, plane = lax.axis_index("z"), lax.axis_index(PLANE_AXES)
    n_plane = lax.axis_size(PLANE_AXES)

    def link_rows(within, first_row, column_lines):
        level, slope, off = column_lines
        level_rows, slope_rows, off_rows = [
            lax.dynamic_slice_in_dim(values, first_row, rows, axis=1) for values in row_lines
        ]
        between = lax.dot_general(
            off_rows,
            off,
            (((0,), (0,)), ((), ())),
            precision=lax.Precision.HIGHEST,
            preferred_element_type=F32,
        )
        link = within * slope * slope_rows[0][:, None] + between / samples_dev
        return (link / total_samples + level_rows[0][:, None] * level).astype(BF16)

    own_rows = link_rows(own_sum, (place * n_plane + plane) * rows, row_lines)
    edge_rows = link_rows(edge_sum, (plane * n_place + place) * rows, lines(next_statistics))
    own = to_all(own_rows, PLANE_AXES).reshape(-1, width)
    own = lax.all_gather(own, "z", axis=0, tiled=True)
    edge = to_all(edge_rows, "z").reshape(-1, width)
    edge = to_all(edge, PLANE_AXES).reshape(-1, width)

    def apply_link(vector):
        ahead = from_next(vector)
        mine = split3(vector)
        lower = from_previous(times(mine, edge, 0))
        result = times(mine, own, 1) + 0.5 * times(split3(ahead), edge, 1)
        return result + 0.5 * lower

    def dots(*pairs):
        local = jnp.stack([jnp.sum(a * b, axis=1) for a, b in pairs])
        opposite = [(i, N_BLOCKS - 1 - i) for i in range(N_BLOCKS)]
        near, far = shift(local, "core", 1), shift(local, "xh", 1)
        across = lax.ppermute(local, BLOCK_AXES, opposite)
        return ((local + near) + (far + across))[:, :, None]

    mask = typed_mask[None, :]
    mask_row = mask.astype(F32)
    scores = z_scores

    residual = mask_row * scores
    residual_link = apply_link(residual)
    image = mask_row * residual_link + RIDGE * residual
    norm_now, curvature = dots((residual, residual), (residual, image))
    image_link = apply_link(image)
    direction, direction_link = residual, residual_link
    push, push_link = image, image_link
    step_size = norm_now / curvature
    solution = step_size * direction
    projected = step_size * direction_link
    for iteration in range(1, ITERS):
        residual = residual - step_size * push
        residual_link = residual_link - step_size * push_link
        image = mask_row * residual_link + RIDGE * residual
        norm_next, fresh, cross_a, cross_b, old, lean, size = dots(
            (residual, residual),
            (residual, image),
            (residual, push),
            (direction, image),
            (direction, push),
            (residual, direction),
            (direction, direction),
        )
        ratio = norm_next / norm_now
        curvature = fresh + ratio * (cross_a + cross_b) + ratio * ratio * old
        length = norm_next + ratio * (2.0 * lean) + ratio * ratio * size
        step_size = norm_next / jnp.maximum(curvature, 0.1 * RIDGE * length)
        if iteration + 1 < ITERS:
            image_link = apply_link(image)
            push_link = image_link + ratio * push_link
            push = image + ratio * push
        direction = residual + ratio * direction
        direction_link = residual_link + ratio * direction_link
        solution = solution + step_size * direction
        projected = projected + step_size * direction_link
        norm_now = norm_next
    imputed = jnp.where(mask == 1, scores, projected)

    return (solution, imputed)


def solution(mesh):
    fine = Mesh(mesh.devices.reshape(SIZES), SAMPLE_AXES + BLOCK_AXES)
    placed = (P(SAMPLE_AXES, BLOCK_AXES), P(BLOCK_AXES), P(SAMPLE_AXES, BLOCK_AXES))

    return jax.shard_map(
        on_device,
        mesh=fine,
        in_specs=placed,
        out_specs=(P(SAMPLE_AXES, BLOCK_AXES), P(SAMPLE_AXES, BLOCK_AXES)),
        check_vma=False,
    )
```

```python
import jax
import jax.numpy as jnp
from jax import lax
from jax.sharding import Mesh, PartitionSpec as P

ITERS = 3
RIDGE = 0.1
EPSILON = 1e-05
BF16 = jnp.bfloat16
F32 = jnp.float32

SAMPLE_AXES = ("z", "y", "xl")
BLOCK_AXES = ("xh", "core")
PLANE_AXES = ("y", "xl")
SIZES = (8, 4, 2, 2, 2)
N_BLOCKS = 4


def shift(block, axis, distance):
    size = lax.axis_size(axis)
    return lax.ppermute(block, axis, [(i, (i + distance) % size) for i in range(size)])


def from_next(block):
    return lax.ppermute(block, BLOCK_AXES, [(i + 1, i) for i in range(N_BLOCKS - 1)])


def from_previous(block):
    return lax.ppermute(block, BLOCK_AXES, [(i, i + 1) for i in range(N_BLOCKS - 1)])


def contract_rows(first_mat, second_mat):
    return lax.dot_general(
        first_mat, second_mat, (((0,), (0,)), ((), ())), preferred_element_type=F32
    )


def rounded(values):
    return lax.reduce_precision(values, exponent_bits=8, mantissa_bits=7)


def split3(vector):
    high = rounded(vector)
    rest = vector - high
    mid = rounded(rest)
    return jnp.concatenate([high, mid, rest - mid], axis=0).astype(BF16)


def times(stacked, matrix, side):
    out = lax.dot_general(
        stacked, matrix, (((1,), (side,)), ((), ())), preferred_element_type=F32
    )
    rows = stacked.shape[0] // 3
    return out[2 * rows :] + out[rows : 2 * rows] + out[:rows]


def add(first, second):
    return (first.astype(F32) + second.astype(F32)).astype(BF16)


def ring_reduce(parts, axis):
    size = lax.axis_size(axis)
    half = size // 2
    here = lax.axis_index(axis).astype(jnp.uint32)

    def part(offset):
        return lax.dynamic_index_in_dim(parts, (here + (offset + size)) & (size - 1), 1, keepdims=False)

    far = part(half)
    right, left = shift(far[:1], axis, 1), shift(far[1:], axis, -1)
    for offset in range(half - 1, 0, -1):
        ahead, behind = part(offset), part(-offset)
        if offset == half - 1:
            ahead = jnp.concatenate([add(ahead[:1], right), ahead[1:]], axis=0)
            behind = jnp.concatenate([behind[:1], add(behind[1:], left)], axis=0)
        else:
            ahead, behind = add(ahead, right), add(behind, left)
        right, left = shift(ahead, axis, 1), shift(behind, axis, -1)
    mine = part(0).astype(F32)
    if half == 1:
        return mine + jnp.concatenate([right, left], axis=0).astype(F32)
    return mine + right.astype(F32) + left.astype(F32)


def exchange(parts, axes):
    return lax.all_to_all(parts, axes, 0, 0, tiled=True)


def to_all(block, axes):
    copies = jnp.broadcast_to(block[None], (lax.axis_size(axes),) + block.shape)
    return exchange(lax.optimization_barrier(copies), axes)


def reduce_over(rows, axes):
    size = lax.axis_size(axes)
    parts = exchange(rows.reshape((size, -1) + rows.shape[1:]), axes)
    return jnp.sum(parts.astype(F32), axis=0)


def line_of(all_sums, all_squares, total_samples):
    coded_sum = jnp.sum(all_sums, axis=0, keepdims=True)
    mean_dosage = (coded_sum + total_samples) / total_samples
    squares = all_squares + 2.0 * coded_sum + total_samples
    variance = squares / total_samples - mean_dosage * mean_dosage
    scale = lax.rsqrt(variance + EPSILON)
    twos = 0.5 * (all_squares + coded_sum)
    zeros = 0.5 * (all_squares - coded_sum)
    ones = total_samples - all_squares
    level = rise = spread = 0.0
    for dosage, count in ((0.0, zeros), (1.0, ones), (2.0, twos)):
        away = dosage - mean_dosage
        value = rounded(away * scale)
        level = level + count * value
        rise = rise + count * value * away
        spread = spread + count * away * away
    slope = jnp.where(spread > 0.0, rise / jnp.where(spread > 0.0, spread, 1.0), scale)
    return level / total_samples, slope


def on_device(genotypes, typed_mask, z_scores):
    samples_dev, width = genotypes.shape
    total_samples = samples_dev * lax.axis_size(SAMPLE_AXES)
    coded = lax.optimization_barrier((genotypes - 1).astype(BF16))
    following = from_next(coded)

    def column_sums(values):
        return jnp.sum(values.astype(F32), axis=0, keepdims=True)

    def centred(row_sums, others, other_sums):
        counts = contract_rows(coded, others)
        return (counts - row_sums[0][:, None] * (other_sums / samples_dev)).astype(BF16)

    sums = column_sums(coded)
    squares = column_sums(coded * coded)
    following_sums = from_next(sums)
    own_part = centred(sums, coded, sums)
    own_sum = lax.psum_scatter(own_part, "z", scatter_dimension=0, tiled=True)

    everyone = to_all(jnp.concatenate([sums, squares], axis=0), ("z", "y"))
    table = jnp.concatenate(
        [everyone[:, 0], jnp.sum(everyone[:, 1], axis=0, keepdims=True)], axis=0
    )
    table, following = lax.optimization_barrier((table, following))
    partner = shift(table, "xl", 1)
    statistics = jnp.concatenate([table[:-1], partner[:-1], table[-1:] + partner[-1:]], axis=0)
    next_statistics = from_next(statistics)

    edge_part = centred(sums, following, following_sums)
    n_place, n_row = lax.axis_size("z"), lax.axis_size("y")
    edge_part = edge_part.reshape(n_row, 2, -1, width).swapaxes(0, 1)
    edge_sum = ring_reduce(edge_part, "y").astype(BF16)
    edge_sum = edge_sum.reshape(2, n_place, -1, width).swapaxes(0, 1).reshape(-1, width)
    edge_sum = reduce_over(edge_sum, "z").astype(BF16)
    edge_sum, own_sum = lax.optimization_barrier((edge_sum, own_sum))
    edge_sum = edge_sum.reshape(2, -1, width)
    side = lax.axis_index("xl").astype(jnp.uint32)
    kept = lax.dynamic_index_in_dim(edge_sum, side, 0, keepdims=False)
    sent = lax.dynamic_index_in_dim(edge_sum, 1 - side, 0, keepdims=False)
    edge_sum = kept.astype(F32) + shift(sent, "xl", 1).astype(F32)
    own_sum = reduce_over(own_sum, PLANE_AXES)

    def lines(table):
        level, slope = line_of(table[:-1], table[-1:], total_samples)
        off = (table[:-1] - jnp.mean(table[:-1], axis=0, keepdims=True)) * slope
        return level, slope, off

    row_lines = lines(statistics)
    rows = own_sum.shape[0]
    place, plane = lax.axis_index("z"), lax.axis_index(PLANE_AXES)
    n_plane = lax.axis_size(PLANE_AXES)

    def link_rows(within, first_row, column_lines):
        level, slope, off = column_lines
        level_rows, slope_rows, off_rows = [
            lax.dynamic_slice_in_dim(values, first_row, rows, axis=1) for values in row_lines
        ]
        between = lax.dot_general(
            off_rows,
            off,
            (((0,), (0,)), ((), ())),
            precision=lax.Precision.HIGHEST,
            preferred_element_type=F32,
        )
        link = within * slope * slope_rows[0][:, None] + between / samples_dev
        return (link / total_samples + level_rows[0][:, None] * level).astype(BF16)

    own_rows = link_rows(own_sum, (place * n_plane + plane) * rows, row_lines)
    edge_rows = link_rows(edge_sum, (plane * n_place + place) * rows, lines(next_statistics))
    own = to_all(own_rows, PLANE_AXES).reshape(-1, width)
    own = lax.all_gather(own, "z", axis=0, tiled=True)
    edge = to_all(edge_rows, "z").reshape(-1, width)
    edge = to_all(edge, PLANE_AXES).reshape(-1, width)

    def apply_link(vector):
        ahead = from_next(vector)
        mine = split3(vector)
        lower = from_previous(times(mine, edge, 0))
        result = times(mine, own, 1) + 0.5 * times(split3(ahead), edge, 1)
        return result + 0.5 * lower

    def dots(*pairs):
        local = jnp.stack([jnp.sum(a * b, axis=1) for a, b in pairs])
        local = local + shift(local, "core", 1)
        return (local + shift(local, "xh", 1))[:, :, None]

    mask = typed_mask[None, :]
    mask_row = mask.astype(F32)
    scores = z_scores

    residual = mask_row * scores
    residual_link = apply_link(residual)
    image = mask_row * residual_link + RIDGE * residual
    norm_now, curvature = dots((residual, residual), (residual, image))
    image_link = apply_link(image)
    direction, direction_link = residual, residual_link
    push, push_link = image, image_link
    step_size = norm_now / curvature
    solution = step_size * direction
    projected = step_size * direction_link
    for iteration in range(1, ITERS):
        residual = residual - step_size * push
        residual_link = residual_link - step_size * push_link
        image = mask_row * residual_link + RIDGE * residual
        norm_next, fresh, cross_a, cross_b, old, lean, size = dots(
            (residual, residual),
            (residual, image),
            (residual, push),
            (direction, image),
            (direction, push),
            (residual, direction),
            (direction, direction),
        )
        ratio = norm_next / norm_now
        curvature = fresh + ratio * (cross_a + cross_b) + ratio * ratio * old
        length = norm_next + ratio * (2.0 * lean) + ratio * ratio * size
        step_size = norm_next / jnp.maximum(curvature, 0.1 * RIDGE * length)
        if iteration + 1 < ITERS:
            image_link = apply_link(image)
            push_link = image_link + ratio * push_link
            push = image + ratio * push
        direction = residual + ratio * direction
        direction_link = residual_link + ratio * direction_link
        solution = solution + step_size * direction
        projected = projected + step_size * direction_link
        norm_now = norm_next
    imputed = jnp.where(mask == 1, scores, projected)

    return (solution, imputed)


def solution(mesh):
    fine = Mesh(mesh.devices.reshape(SIZES), SAMPLE_AXES + BLOCK_AXES)
    placed = (P(SAMPLE_AXES, BLOCK_AXES), P(BLOCK_AXES), P(SAMPLE_AXES, BLOCK_AXES))

    return jax.shard_map(
        on_device,
        mesh=fine,
        in_specs=placed,
        out_specs=(P(SAMPLE_AXES, BLOCK_AXES), P(SAMPLE_AXES, BLOCK_AXES)),
        check_vma=False,
    )
```
